32 devices in a mesh: grp: 2 (over x), tp: 8 (over z, y), role: 2 (over core).
Axes of the slice: x: 2, y: 2, z: 4, core: 2. Of those that a mesh axis runs over, the one named last changes fastest.
Arguments:
- prompt_states: bfloat16 [2048, 8192], P(('grp', 'role'), 'tp'), parts along dimension 0, may hold values from -80 to 80
- kv_weight: bfloat16 [8192, 2048], P('tp'), may hold values from -0.0625 to 0.0625
- prompt_segments: int32 [4, 512], P(('grp', 'role')), parts along dimension 0, may hold values from 0 to 7, never falling along the last dimension, each value on 1 to 128 neighbouring positions
- page_dest: int32 [4, 4], P(('grp', 'role')), parts along dimension 0, may hold values from 0 to 7, as said below
- new_slot: int32 [4, 4], P(('grp', 'role')), parts along dimension 0, may hold values from 0 to 7, as said below
- cache_keys: bfloat16 [4, 64, 8, 128, 128], P(('grp', 'role'), 'tp'), parts along dimension 0, may hold values from -6 to 6
- cache_values: bfloat16 [4, 64, 8, 128, 128], P(('grp', 'role'), 'tp'), parts along dimension 0, may hold values from -6 to 6
- decode_queries: bfloat16 [4, 8, 8192], P(('grp', 'role')), parts along dimension 0, may hold values from -400 to 400
- request_pages: int32 [4, 8, 8], P(('grp', 'role')), parts along dimension 0, may hold values from 0 to 63, as said below
- context_lengths: int32 [4, 8], P(('grp', 'role')), parts along dimension 0, may hold values from 130 to 1024, as said below
- out_weight: bfloat16 [8192, 8192], P(None, 'tp'), may hold values from -1 to 1
Outputs:
- attention_out: bfloat16 [4, 8, 8192], P(('grp', 'role'), None, 'tp'), parts along dimension 0
The draws below stay inside these ranges and needn't reach their ends.
There are 2 independent parts, one for each index of `grp`. The reference program is written for one: setup_inputs(seed, part) draws one part's arguments, and reference() takes and returns one part's arrays. A program takes and returns all parts, laid end to end along the dimension named above; an argument that names none is the same for every part. Nothing has to cross between parts.
Inputs may be any that keep to these rules, and one draw needn't show every extreme that they name: `page_dest`: no decode device receives more than 2 prompt pages; in each sub-replica some device receives exactly 2. `new_slot`: prompt pages that go to the same device have different slots. `request_pages`: in each sub-replica every pool page 0 to 63 appears exactly once among the 8 x 8 entries; every page that receives a prompt page stands at an entry below 1 of its list. `context_lengths`: in each sub-replica some request has exactly 1024 tokens.
All inputs are finite; a program needn't handle non-finite values.
Results may differ from the reference program's by a relative error of at most 0.024.
Values may be sent and summed in bfloat16 or wider, within the bound.
A program may use at most 128 MiB of HBM per device.

```python
import math
import jax
import jax.numpy as jnp
import numpy as np
from jax import lax

D = 8192
QH = 64
KVH = 8
HD = 128
PAGE = 128
CAPR = 2
POOL_DEV = 8
B = 8
NPG = 4
PTOK = 512
NPOOL = 64
MAXP = 8
NEWK = 1
N_TP = 8


def page_tables(key):
    seat_key, lucky_key, order_key, slot_key, score_key, length_key, pick_key = jax.random.split(jax.random.fold_in(key, 17), 7)
    seats = N_TP * CAPR
    seat_ids = jnp.arange(seats, dtype=jnp.int32)
    lucky = jax.random.randint(lucky_key, (2, 1), 0, N_TP, jnp.int32)
    seat_noise = jax.random.randint(seat_key, (2, seats), 0, seats, jnp.int32)
    priority = jnp.where((seat_ids // CAPR)[None, :] == lucky, 0, 1)
    seat_scores = (priority * seats + seat_noise) * seats + seat_ids[None, :]
    chosen = jnp.argsort(seat_scores, axis=1, stable=True).astype(jnp.int32)[:, :NPG]
    order_noise = jax.random.randint(order_key, (2, NPG), 0, NPG, jnp.int32)
    order = jnp.argsort(order_noise * NPG + jnp.arange(NPG, dtype=jnp.int32)[None, :], axis=1, stable=True).astype(jnp.int32)
    chosen = jnp.take_along_axis(chosen, order, axis=1)
    page_dest = chosen // CAPR
    slot_noise = jax.random.randint(slot_key, (2, N_TP, POOL_DEV), 0, POOL_DEV, jnp.int32)
    slot_perm = jnp.argsort(slot_noise * POOL_DEV + jnp.arange(POOL_DEV, dtype=jnp.int32)[None, None, :], axis=2, stable=True).astype(jnp.int32)
    new_slot = jnp.take_along_axis(slot_perm.reshape(2, N_TP * POOL_DEV), page_dest * POOL_DEV + chosen % CAPR, axis=1)
    targets = page_dest * POOL_DEV + new_slot
    page_ids = jnp.arange(NPOOL, dtype=jnp.int32)
    is_new = jnp.any(targets[:, :, None] == page_ids[None, None, :], axis=1)
    noise = jax.random.randint(score_key, (2, NPOOL), 0, NPOOL, jnp.int32)
    scores = (noise + jnp.where(is_new, 0, NPOOL)) * NPOOL + page_ids[None, :]
    ordered = jnp.argsort(scores, axis=1, stable=True).astype(jnp.int32)
    page_lists = ordered.reshape(2, MAXP, B).transpose(0, 2, 1)
    lengths = jax.random.randint(length_key, (2, B), NEWK * PAGE + 2, MAXP * PAGE + 1, jnp.int32)
    longest = jax.random.randint(pick_key, (2, 1), 0, B, jnp.int32)
    lengths = jnp.where(jnp.arange(B, dtype=jnp.int32)[None, :] == longest, MAXP * PAGE, lengths)
    return (page_dest, new_slot, page_lists, lengths)


def draw_prompt_states(key, part):
    column_key, base_key = jax.random.split(jax.random.fold_in(key, 5), 2)
    column_scale = jnp.exp(jax.random.uniform(column_key, (1, D), jnp.float32, 0.0, math.log(10.0)))
    ramp = jnp.arange(D, dtype=jnp.float32)[None, :] / D
    base = jnp.clip(jax.random.normal(base_key, (2 * PTOK, D), jnp.float32), -4.0, 4.0)
    rising = 3.0 ** ramp
    scale = column_scale * rising
    scale = scale / jnp.sqrt(jnp.mean(scale * scale))
    return (base * scale).astype(jnp.bfloat16)


def draw_page_dest(key, part):
    return page_tables(key)[0]


def draw_new_slot(key, part):
    return page_tables(key)[1]


def draw_request_pages(key, part):
    return page_tables(key)[2]


def draw_context_lengths(key, part):
    return page_tables(key)[3]


def draw_decode_queries(key, part):
    base = jnp.clip(jax.random.normal(jax.random.fold_in(key, 23), (2, B, QH * HD), jnp.float32), -4.0, 4.0)
    return base.astype(jnp.bfloat16)


def draw_cache_keys(key, part):
    shape = (2, NPOOL, KVH, PAGE, HD)
    base = jnp.clip(jax.random.normal(jax.random.fold_in(key, 37), shape, jnp.float32), -6.0, 6.0)
    return base.astype(jnp.bfloat16)


def steps_of(stream_key, extent, cuts, least, high):
    loudness, own = 1.0, jax.random.fold_in(stream_key, 6)
    for position, parts in cuts:
        steps = jnp.exp(jax.random.uniform(jax.random.fold_in(own, position), (parts,), jnp.float32, least / len(cuts), high / len(cuts)))
        loudness = loudness * jnp.repeat(steps, extent[position] // parts).reshape([-1 if axis == position else 1 for axis in range(len(extent))])
    return loudness


def length_profile(amount, total, bound, lean):
    portions = [(1 << 20) // math.isqrt(grade ** lean) + 1 for grade in range(2, amount + 1)]
    rest, given = total - bound - (amount - 1), [1] * (amount - 1)
    while rest > 0:
        candidates = [i for i in range(amount - 1) if given[i] < bound]
        mass, budget = sum([portions[i] for i in candidates]), rest
        for i in candidates:
            addition = min(bound - given[i], max(1, budget * portions[i] // mass), rest)
            given[i] = given[i] + addition
            rest = rest - addition
    return np.array([bound] + given)


def ragged(key, amount, total, most, skew):
    if amount == 2:
        one = jax.random.randint(key, (), max(1, total - most), min(most, total - 1) + 1)
        return jnp.stack([one, total - one])
    sizes = jnp.asarray(length_profile(amount, total, most, skew), jnp.int32)
    pairs = (amount - 1) // 2
    giver, taker = sizes[1:1 + 2 * pairs:2], sizes[2:2 + 2 * pairs:2]
    room = jnp.minimum(giver - 1, most - taker)
    shifted = jax.random.randint(jax.random.fold_in(key, 1), (pairs,), 0, 1 << 20) % (room + 1)
    sizes = sizes.at[1:1 + 2 * pairs:2].set(giver - shifted).at[2:2 + 2 * pairs:2].set(taker + shifted)
    return sizes[jax.random.permutation(jax.random.fold_in(key, 2), amount)]


def gaussian(rng, dims, width, limit, shards=(), held_as=jnp.bfloat16):
    values = width * jax.random.normal(rng, dims, jnp.float32)
    if shards:
        values = values * steps_of(rng, dims, shards, -0.22, 0.18)
    return jnp.clip(values, -limit, limit).astype(held_as)


def setup_inputs(seed: int = 0, part: int = 0) -> dict:
    key_list = jax.random.split(jax.random.key(seed), 12)
    part_splits = jax.random.split(jax.random.fold_in(key_list[11], part), 12)
    prompt_states = draw_prompt_states(jax.random.fold_in(jax.random.fold_in(key_list[11], part), 71), part)
    kv_weight = gaussian(key_list[1], (D, 2 * KVH * HD), D ** -0.5, 0.0625, ((0, 8),))
    prompt_segments = jax.vmap(lambda own: jnp.searchsorted(jnp.cumsum(ragged(own, 8, PTOK, PTOK // 4, 2)), jnp.arange(PTOK), side="right"))(jax.random.split(part_splits[2], 2)).reshape((2, PTOK)).astype(jnp.int32)
    page_dest = draw_page_dest(jax.random.fold_in(jax.random.fold_in(key_list[11], part), 71), part)
    new_slot = draw_new_slot(jax.random.fold_in(jax.random.fold_in(key_list[11], part), 71), part)
    cache_keys = draw_cache_keys(jax.random.fold_in(jax.random.fold_in(key_list[11], part), 71), part)
    cache_values = gaussian(part_splits[6], (2, NPOOL, KVH, PAGE, HD), 1.0, 6.0, ((0, 2), (1, 8)))
    decode_queries = draw_decode_queries(jax.random.fold_in(jax.random.fold_in(key_list[11], part), 71), part)
    request_pages = draw_request_pages(jax.random.fold_in(jax.random.fold_in(key_list[11], part), 71), part)
    context_lengths = draw_context_lengths(jax.random.fold_in(jax.random.fold_in(key_list[11], part), 71), part)
    out_weight = gaussian(key_list[10], (QH * HD, D), (4 * max(1, QH * HD // (MAXP * PAGE))) ** -0.5, 1.0, ((1, 8),))
    return dict(prompt_states=prompt_states, kv_weight=kv_weight, prompt_segments=prompt_segments, page_dest=page_dest, new_slot=new_slot, cache_keys=cache_keys, cache_values=cache_values, decode_queries=decode_queries, request_pages=request_pages, context_lengths=context_lengths, out_weight=out_weight)


rope_base = 500000.0
neg_fill = -1e+30

def rotate(key_heads, positions):
    half_width = key_heads.shape[-1] // 2
    frequency = rope_base ** (-(jnp.arange(half_width, dtype=jnp.float32) * 2.0) / key_heads.shape[-1])
    angles = positions.astype(jnp.float32)[:, None] * frequency[None, :]
    cosine = jnp.cos(angles)[:, None, :]
    sine_part = jnp.sin(angles)[:, None, :]
    lower_half = key_heads[..., :half_width]
    upper_half = key_heads[..., half_width:]
    return jnp.concatenate([lower_half * cosine - upper_half * sine_part, upper_half * cosine + lower_half * sine_part], axis=-1)

def page_partials(owned_queries, key_pages, value_pages, page_limit):
    page_count, head_count, page_width, head_depth = key_pages.shape
    grouped = owned_queries.reshape(page_count, head_count, -1, head_depth)
    scores = jnp.einsum('pgqd,pgtd->pgqt', grouped.astype(jnp.float32), key_pages.astype(jnp.float32)) * (1.0 / math.sqrt(head_depth))
    is_live = jnp.arange(page_width)[None, None, None, :] < page_limit[:, None, None, None]
    page_max = lax.optimization_barrier(jnp.max(jnp.where(is_live, scores, neg_fill), axis=-1))
    weights = jnp.exp(jnp.where(is_live, scores - page_max[..., None], neg_fill)).astype(jnp.bfloat16)
    page_sum = lax.optimization_barrier(jnp.sum(weights.astype(jnp.float32), axis=-1))
    page_acc = jnp.einsum('pgqt,pgtd->pgqd', weights.astype(jnp.float32), value_pages.astype(jnp.float32))
    all_heads = head_count * grouped.shape[2]
    return (page_max.reshape(page_count, all_heads), page_sum.reshape(page_count, all_heads), page_acc.reshape(page_count, all_heads, head_depth))

def join_pages(page_max, page_sum, page_acc, page_lists):
    chosen_max = page_max[page_lists]
    largest = lax.optimization_barrier(jnp.max(chosen_max, axis=1))
    factor = jnp.exp(chosen_max - largest[:, None, :])
    grand_sum = lax.optimization_barrier(jnp.sum(factor * page_sum[page_lists], axis=1))
    numerator = jnp.einsum('bkh,bkhd->bhd', factor, page_acc[page_lists], precision=lax.Precision.HIGHEST)
    return (numerator / grand_sum[..., None]).astype(jnp.bfloat16).reshape(page_lists.shape[0], -1)

def reference(prompt_states, kv_weight, prompt_segments, page_dest, new_slot, cache_keys, cache_values, decode_queries, request_pages, context_lengths, out_weight):
    normed = prompt_states
    block_width = D // N_TP
    columns = kv_weight.shape[1]

    def add_block(running, block_index):
        row_block = lax.dynamic_slice_in_dim(normed, block_index * block_width, block_width, 1)
        weight = lax.dynamic_slice_in_dim(kv_weight, block_index * block_width, block_width, 0)
        product = jnp.dot(row_block, weight, preferred_element_type=jnp.float32).astype(jnp.bfloat16)
        product = lax.optimization_barrier(product)
        return (running + product.astype(jnp.float32), None)
    kv_sum, _ = lax.scan(add_block, jnp.zeros((normed.shape[0], columns), jnp.float32), jnp.arange(N_TP, dtype=jnp.int32))
    token_order = jnp.arange(PTOK, dtype=jnp.int32)
    same_prompt = (prompt_segments[:, :, None] == prompt_segments[:, None, :]) & (token_order[None, None, :] < token_order[None, :, None])
    positions = lax.optimization_barrier(jnp.sum(same_prompt.astype(jnp.int32), axis=2))
    kv_sum = kv_sum.reshape(2, PTOK, 2, KVH, HD)
    new_keys = jax.vmap(rotate)(kv_sum[:, :, 0], positions).astype(jnp.bfloat16)
    new_values = kv_sum[:, :, 1].astype(jnp.bfloat16)
    key_pages = new_keys.reshape(2, NPG, PAGE, KVH, HD).transpose(0, 1, 3, 2, 4)
    value_pages = new_values.reshape(2, NPG, PAGE, KVH, HD).transpose(0, 1, 3, 2, 4)
    targets = page_dest * POOL_DEV + new_slot
    role_index = jnp.arange(2)[:, None]
    pool_keys = cache_keys.at[role_index, targets].set(key_pages)
    pool_values = cache_values.at[role_index, targets].set(value_pages)
    entry_index = jnp.arange(MAXP, dtype=jnp.int32)
    limits = context_lengths[:, :, None] - entry_index[None, None, :] * PAGE
    flat_pages = request_pages.reshape(2, -1)
    page_limit = jnp.zeros((2, NPOOL), jnp.int32).at[role_index, flat_pages].set(limits.reshape(2, -1))
    owner_ids = jnp.broadcast_to(jnp.arange(B, dtype=jnp.int32)[None, :, None], (2, B, MAXP)).reshape(2, -1)
    owners = jnp.zeros((2, NPOOL), jnp.int32).at[role_index, flat_pages].set(owner_ids)
    owned_queries = jnp.take_along_axis(decode_queries, owners[:, :, None], axis=1)
    page_max, page_sum, page_acc = jax.vmap(page_partials)(owned_queries, pool_keys, pool_values, page_limit)
    attention = jax.vmap(join_pages)(page_max, page_sum, page_acc, request_pages)
    result = jnp.dot(attention.reshape(2 * B, QH * HD), out_weight, preferred_element_type=jnp.float32)
    return result.astype(jnp.bfloat16).reshape(2, B, D)
```

```python
import functools
import math

import jax
import jax.numpy as jnp
import numpy as np
from jax import lax
from jax.experimental import pallas as pl
from jax.experimental.pallas import tpu as pltpu
from jax.sharding import PartitionSpec as P

KVH = 8
HD = 128


rope_base = 500000.0
neg_fill = -1e30


def cos_turn_coefficients():
    nodes = 0.125 * (1.0 + np.cos((np.arange(400) + 0.5) * np.pi / 400))
    basis = np.polynomial.chebyshev.Chebyshev.fit(
        nodes, np.cos(2.0 * np.pi * np.sqrt(nodes)), 8, domain=[0.0, 0.25]
    )
    return [float(c) for c in basis.convert(kind=np.polynomial.Polynomial).coef]


def rotation_tables(seg_row, tokens, width):
    index = lax.broadcasted_iota(jnp.int32, (tokens, width), 0)
    start = jnp.zeros((tokens, width), jnp.int32)
    for value in range(1, 8):
        first = jnp.sum((seg_row < value).astype(jnp.int32), axis=1, keepdims=True)
        start = jnp.maximum(start, jnp.where(first <= index, first, 0))
    position = (index - start).astype(jnp.float32)
    lane = lax.broadcasted_iota(jnp.int32, (1, width), 1)
    half = width // 2
    low = lane < half
    exponent = jnp.where(low, lane, lane - half).astype(jnp.float32) * (2.0 / width)
    turns = jnp.exp(exponent * (-math.log(rope_base))) * (1.0 / (2.0 * math.pi))
    phase = position * turns
    phase = phase - jnp.round(phase)
    phase = phase - jnp.where(low, 0.0, 0.25)
    phase = phase - jnp.round(phase)
    square = phase * phase
    coefficients = cos_turn_coefficients()
    value = jnp.full_like(square, coefficients[-1])
    for c in coefficients[-2::-1]:
        value = value * square + c
    turned = pltpu.roll(value, half, 1)
    return jnp.where(low, value, turned), jnp.where(low, turned, value)


def fused_kernel(
    ranks,
    x_hbm,
    w_hbm,
    seg_ref,
    dest_ref,
    slot_ref,
    kc_hbm,
    vc_hbm,
    q_ref,
    rp_ref,
    len_ref,
    ow_hbm,
    out_ref,
    x_v,
    wk_v,
    wv_v,
    kc_v,
    vc_v,
    ow_v,
    v_new,
    q_all,
    qp,
    cos_v,
    sin_v,
    live_v,
    s_send,
    s_recv,
    w_all,
    num_send,
    num_recv,
    stat_send,
    stat_recv,
    acc_send,
    acc_recv,
    att_all,
    x_sem,
    wk_sem,
    wv_sem,
    kc_sem,
    vc_sem,
    ow_sem,
    tx,
    rx,
):
    me = lax.axis_index("tp")
    tokens, features = x_v.shape
    pools = kc_hbm.shape[1]
    pages = dest_ref.shape[1]
    page = kc_hbm.shape[3]
    requests = q_ref.shape[1]
    group = q_ref.shape[2] // (KVH * HD)
    rows = group * requests
    chunk = ow_v.shape[1]
    scale = 1.0 / math.sqrt(HD)
    halves = KVH // 2

    barrier = pltpu.get_barrier_semaphore()
    for d in range(1, ranks):
        pl.semaphore_signal(barrier, inc=1, device_id={"tp": lax.rem(me + d, ranks)})

    def pair_of(i):
        return lax.rem(me // 2 + 1 + i, halves)

    def head_of(i):
        return lax.rem(me + 1 + i, ranks)

    def x_copy():
        return pltpu.make_async_copy(x_hbm, x_v, x_sem)

    def wk_copy(i):
        return pltpu.make_async_copy(
            w_hbm.at[:, pl.ds(pl.multiple_of(pair_of(i) * (2 * HD), 2 * HD), 2 * HD)],
            wk_v.at[i],
            wk_sem.at[i],
        )

    def wv_copy(i):
        return pltpu.make_async_copy(
            w_hbm.at[:, pl.ds(pl.multiple_of((halves + i) * (2 * HD), 2 * HD), 2 * HD)],
            wv_v.at[i],
            wv_sem.at[i],
        )

    def kc_copy(i):
        return pltpu.make_async_copy(
            kc_hbm.at[0, i], kc_v.at[:, pl.ds(i * page, page), :], kc_sem.at[i]
        )

    def vc_copy(i):
        return pltpu.make_async_copy(
            vc_hbm.at[0, i], vc_v.at[:, pl.ds(i * page, page), :], vc_sem.at[i]
        )

    def ow_copy(i):
        return pltpu.make_async_copy(
            ow_hbm.at[pl.ds(i * chunk, chunk), :], ow_v.at[i], ow_sem.at[i]
        )

    x_copy().start()
    for i in range(halves):
        wk_copy(i).start()
    for i in range(halves):
        wv_copy(i).start()
    for i in range(pools):
        kc_copy(i).start()
    for i in range(pools):
        vc_copy(i).start()

    def remote(kind, src, dst, peer):
        return pltpu.make_async_remote_copy(
            src_ref=src,
            dst_ref=dst,
            send_sem=tx.at[kind, peer],
            recv_sem=rx.at[kind, me],
            device_id={"tp": peer},
        )

    def score_send(peer):
        return remote(0, s_send.at[peer], s_recv.at[me], peer)

    def weight_send(peer):
        return remote(1, w_all.at[me], w_all.at[me], peer)

    def num_copy(peer):
        return remote(2, num_send.at[peer], num_recv.at[me], peer)

    def stat_copy(peer):
        return remote(3, stat_send.at[peer], stat_recv.at[me], peer)

    def acc_copy(peer):
        return remote(4, acc_send.at[peer], acc_recv.at[me], peer)

    def att_copy(peer):
        return remote(5, att_all.at[me], att_all.at[me], peer)

    def arrival(kind, ref, source):
        pltpu.make_async_remote_copy(
            src_ref=ref.at[source],
            dst_ref=ref.at[source],
            send_sem=tx.at[kind, source],
            recv_sem=rx.at[kind, source],
            device_id={"tp": source},
        ).wait_recv()

    lists = rp_ref[0]
    longest = lists.shape[1]
    entry = lax.broadcasted_iota(jnp.int32, (requests, longest), 1)
    request = lax.broadcasted_iota(jnp.int32, (requests, longest), 0)
    length = jnp.zeros((requests, longest), jnp.int32)
    for r in range(requests):
        length = jnp.where(request == r, len_ref[0, r], length)
    limit = length - entry * page

    targets = [dest_ref[0, p] * pools + slot_ref[0, p] for p in range(pages)]
    token = lax.broadcasted_iota(jnp.int32, (requests, page), 1)
    for s in range(pools):
        g = me * pools + s
        kept = jnp.int32(1)
        for p in range(pages):
            kept = jnp.where(targets[p] == g, 0, kept)
        bound = jnp.sum(jnp.where(lists == g, limit * kept, 0), axis=1, keepdims=True)
        live_v[:, s * page : (s + 1) * page] = jnp.where(token < bound, 1.0, 0.0)
    owners, bounds = [], []
    for p in range(pages):
        hit = lists == targets[p]
        owners.append(jnp.sum(jnp.where(hit, request, 0), keepdims=True))
        bounds.append(jnp.sum(jnp.where(hit, limit, 0), keepdims=True))

    q_rows = q_ref[0].astype(jnp.float32)
    lane = lax.broadcasted_iota(jnp.int32, (1, HD), 1)
    sign = jnp.where(lane < HD // 2, 1.0, -1.0)
    pick_row = lax.broadcasted_iota(jnp.int32, (pages * group, rows), 0)
    pick_col = lax.broadcasted_iota(jnp.int32, (pages * group, rows), 1)
    owner_rows = jnp.zeros((pages * group, rows), jnp.int32)
    for p in range(pages):
        owner_rows = jnp.where(pick_row // group == p, owners[p], owner_rows)
    pick = jnp.where(pick_col == (pick_row % group) * requests + owner_rows, 1.0, 0.0).astype(
        jnp.bfloat16
    )
    for h in range(KVH):
        part = jnp.concatenate(
            [
                q_rows[:, (h * group + k) * HD : (h * group + k + 1) * HD]
                for k in range(group)
            ],
            axis=0,
        )
        both = jnp.concatenate([part, pltpu.roll(part, HD // 2, 1) * sign], axis=1).astype(
            jnp.bfloat16
        )
        q_all[h] = both
        qp[h] = jnp.dot(pick, both, preferred_element_type=jnp.float32).astype(jnp.bfloat16)

    cosine, sine = rotation_tables(seg_ref[...], tokens, HD)
    cos_v[...] = cosine
    sin_v[...] = sine

    pl.semaphore_wait(barrier, ranks - 1)
    x_copy().wait()

    @pl.loop(0, halves)
    def _(i):
        wk_copy(i).wait()
        product = jnp.dot(x_v[...], wk_v[i], preferred_element_type=jnp.float32)
        for j in range(2):
            h = pair_of(i) * 2 + j
            keys = product[:, j * HD : (j + 1) * HD]
            turned = jnp.concatenate([keys * cos_v[...], keys * sin_v[...]], axis=1).astype(
                jnp.bfloat16
            )
            scores = lax.dot_general(
                qp[h], turned, (((1,), (1,)), ((), ())), preferred_element_type=jnp.float32
            )
            for p in range(pages):
                s_send[h, :, p * page : (p + 1) * page] = (
                    scores[p * group : (p + 1) * group, p * page : (p + 1) * page] * scale
                )

            @pl.when(h != me)
            def _():
                score_send(h).start()

    for i in range(ranks):
        ow_copy(i).start()

    @pl.loop(0, halves)
    def _(i):
        wv_copy(i).wait()
        product = jnp.dot(x_v[...], wv_v[i], preferred_element_type=jnp.float32)
        for j in range(2):
            v_new[i * 2 + j] = product[:, j * HD : (j + 1) * HD].astype(jnp.bfloat16)

    total_scores = s_send[me]
    for d in range(1, ranks):
        source = lax.rem(me + d, ranks)
        arrival(0, s_recv, source)
        total_scores = total_scores + s_recv[source]
    page_token = lax.broadcasted_iota(jnp.int32, (group, page), 1)
    new_max, new_sum = [], []
    for p in range(pages):
        alive = page_token < bounds[p]
        scores = total_scores[:, p * page : (p + 1) * page]
        top = jnp.max(jnp.where(alive, scores, neg_fill), axis=1, keepdims=True)
        weight = jnp.exp(jnp.where(alive, scores - top, neg_fill)).astype(jnp.bfloat16)
        w_all[me, :, p * page : (p + 1) * page] = weight
        new_max.append(top)
        new_sum.append(jnp.sum(weight.astype(jnp.float32), axis=1, keepdims=True))
    for d in range(1, ranks):
        weight_send(lax.rem(me + d, ranks)).start()

    for i in range(pools):
        kc_copy(i).wait()
    for i in range(pools):
        vc_copy(i).wait()
    stat_lane = lax.broadcasted_iota(jnp.int32, (rows, HD), 1)

    def resident(i, stats):
        h = head_of(i)
        scores = (
            lax.dot_general(
                q_all[h][:, :HD],
                kc_v[h],
                (((1,), (1,)), ((), ())),
                preferred_element_type=jnp.float32,
            )
            * scale
        )
        mask = jnp.concatenate([live_v[...]] * group, axis=0) > 0.5
        top = jnp.max(jnp.where(mask, scores, neg_fill), axis=1, keepdims=True)
        weight = jnp.where(mask, jnp.exp(jnp.where(mask, scores - top, 0.0)), 0.0).astype(
            jnp.bfloat16
        )
        total = jnp.sum(weight.astype(jnp.float32), axis=1, keepdims=True)
        num_send[h] = jnp.dot(weight, vc_v[h], preferred_element_type=jnp.float32).astype(
            jnp.bfloat16
        )

        @pl.when(h != me)
        def _():
            num_copy(h).start()

        stats = jnp.where(stat_lane == h, top, stats)
        return jnp.where(stat_lane == h + KVH, total, stats)

    stats = lax.fori_loop(0, KVH, resident, jnp.zeros((rows, HD), jnp.float32))
    padded = jnp.concatenate([stats, jnp.zeros((HD - rows, HD), jnp.float32)], axis=0)
    flipped = jnp.transpose(padded)
    for h in range(KVH):
        stat_send[h, 0:1, :] = flipped[h : h + 1, :]
        stat_send[h, 1:2, :] = flipped[KVH + h : KVH + h + 1, :]
    for d in range(1, ranks):
        stat_copy(lax.rem(me + d, ranks)).start()

    @pl.loop(0, ranks)
    def _(i):
        h = lax.rem(me + i, ranks)

        @pl.when(h != me)
        def _():
            arrival(1, w_all, h)

        weight = w_all[h]
        values = v_new[h]
        acc_send[h] = jnp.concatenate(
            [
                jnp.dot(
                    weight[:, p * page : (p + 1) * page],
                    values[p * page : (p + 1) * page],
                    preferred_element_type=jnp.float32,
                )
                for p in range(pages)
            ],
            axis=0,
        ).astype(jnp.bfloat16)

        @pl.when(h != me)
        def _():
            acc_copy(h).start()

    source_row = lax.broadcasted_iota(jnp.int32, (HD, HD), 0)
    for d in range(1, ranks):
        arrival(3, stat_recv, lax.rem(me + d, ranks))
    maxima = jnp.zeros((HD, HD), jnp.float32)
    for d in range(ranks):
        block = stat_send[me] if d == 0 else stat_recv[lax.rem(me + d, ranks)]
        maxima = jnp.where(source_row == d, block[0:1, :], maxima)
        maxima = jnp.where(source_row == d + ranks, block[1:2, :], maxima)
    columns = jnp.transpose(maxima)[:rows]
    old_max = [columns[:, d : d + 1] for d in range(ranks)]
    old_sum = [columns[:, ranks + d : ranks + d + 1] for d in range(ranks)]
    row_request = lax.broadcasted_iota(jnp.int32, (rows, HD), 0) % requests

    def spread(value):
        wide = jnp.broadcast_to(value, (group, HD))
        return jnp.broadcast_to(wide[:, None, :], (group, requests, HD)).reshape(rows, HD)

    mine = [row_request == owners[p] for p in range(pages)]
    fresh_max = [jnp.where(mine[p], spread(new_max[p]), neg_fill) for p in range(pages)]
    top = fresh_max[0]
    for value in fresh_max[1:] + old_max:
        top = jnp.maximum(top, value)
    total = jnp.zeros((rows, HD), jnp.float32)
    numer = jnp.zeros((rows, HD), jnp.float32)
    for d in range(ranks):
        source = lax.rem(me + d, ranks)
        if d:
            arrival(2, num_recv, source)
        factor = jnp.exp(old_max[d] - top)
        total = total + factor * old_sum[d]
        block = num_send[me] if d == 0 else num_recv[source]
        numer = numer + factor * block.astype(jnp.float32)
    fresh_factor = [
        jnp.where(mine[p], jnp.exp(fresh_max[p] - top), 0.0) for p in range(pages)
    ]
    for p in range(pages):
        total = total + fresh_factor[p] * spread(new_sum[p])
    fresh_acc = acc_send[me].astype(jnp.float32)
    for d in range(1, ranks):
        source = lax.rem(me + d, ranks)
        arrival(4, acc_recv, source)
        fresh_acc = fresh_acc + acc_recv[source].astype(jnp.float32)
    for p in range(pages):
        numer = numer + fresh_factor[p] * spread(fresh_acc[p * group : (p + 1) * group])
    joined = (numer / total).astype(jnp.bfloat16)
    for k in range(group):
        att_all[me, :, k * HD : (k + 1) * HD] = joined[k * requests : (k + 1) * requests]
    for d in range(1, ranks):
        att_copy(lax.rem(me + d, ranks)).start()

    for i in range(ranks):
        ow_copy(i).wait()

    def project(i, result):
        source = lax.rem(me + i, ranks)

        @pl.when(source != me)
        def _():
            arrival(5, att_all, source)

        return result + jnp.dot(
            att_all[source], ow_v[source], preferred_element_type=jnp.float32
        )

    result = lax.fori_loop(
        0, ranks, project, jnp.zeros((requests, ow_v.shape[2]), jnp.float32)
    )
    out_ref[0] = result.astype(out_ref.dtype)

    for d in range(1, ranks):
        peer = lax.rem(me + d, ranks)
        score_send(peer).wait_send()
        weight_send(peer).wait_send()
        num_copy(peer).wait_send()
        stat_copy(peer).wait_send()
        acc_copy(peer).wait_send()
        att_copy(peer).wait_send()


def fused(
    prompt_states,
    kv_weight,
    prompt_segments,
    page_dest,
    new_slot,
    cache_keys,
    cache_values,
    decode_queries,
    request_pages,
    context_lengths,
    out_weight,
):
    ranks = lax.axis_size("tp")
    tokens, features = prompt_states.shape
    pools, page = cache_keys.shape[1], cache_keys.shape[3]
    pages = page_dest.shape[1]
    requests = decode_queries.shape[1]
    group = decode_queries.shape[2] // (KVH * HD)
    rows = group * requests
    chunk = out_weight.shape[0] // ranks
    width = out_weight.shape[1]
    half = KVH // 2
    vmem = pl.BlockSpec(memory_space=pltpu.VMEM)
    smem = pl.BlockSpec(memory_space=pltpu.SMEM)
    hbm = pl.BlockSpec(memory_space=pl.ANY)
    bf16, f32 = jnp.bfloat16, jnp.float32
    return pl.pallas_call(
        functools.partial(fused_kernel, ranks),
        out_shape=jax.ShapeDtypeStruct((1, requests, width), bf16),
        in_specs=[hbm, hbm, vmem, smem, smem, hbm, hbm, vmem, vmem, smem, hbm],
        out_specs=vmem,
        scratch_shapes=[
            pltpu.VMEM((tokens, features), bf16),
            pltpu.VMEM((half, features, 2 * HD), bf16),
            pltpu.VMEM((half, features, 2 * HD), bf16),
            pltpu.VMEM((KVH, pools * page, HD), bf16),
            pltpu.VMEM((KVH, pools * page, HD), bf16),
            pltpu.VMEM((ranks, chunk, width), bf16),
            pltpu.VMEM((KVH, tokens, HD), bf16),
            pltpu.VMEM((KVH, rows, 2 * HD), bf16),
            pltpu.VMEM((KVH, pages * group, 2 * HD), bf16),
            pltpu.VMEM((tokens, HD), f32),
            pltpu.VMEM((tokens, HD), f32),
            pltpu.VMEM((requests, pools * page), f32),
            pltpu.VMEM((ranks, group, tokens), f32),
            pltpu.VMEM((ranks, group, tokens), f32),
            pltpu.VMEM((ranks, group, tokens), bf16),
            pltpu.VMEM((ranks, rows, HD), bf16),
            pltpu.VMEM((ranks, rows, HD), bf16),
            pltpu.VMEM((ranks, 8, HD), f32),
            pltpu.VMEM((ranks, 8, HD), f32),
            pltpu.VMEM((ranks, pages * group, HD), bf16),
            pltpu.VMEM((ranks, pages * group, HD), bf16),
            pltpu.VMEM((ranks, requests, chunk), bf16),
            pltpu.SemaphoreType.DMA,
            pltpu.SemaphoreType.DMA((half,)),
            pltpu.SemaphoreType.DMA((half,)),
            pltpu.SemaphoreType.DMA((pools,)),
            pltpu.SemaphoreType.DMA((pools,)),
            pltpu.SemaphoreType.DMA((ranks,)),
            pltpu.SemaphoreType.DMA((6, ranks)),
            pltpu.SemaphoreType.DMA((6, ranks)),
        ],
        compiler_params=pltpu.CompilerParams(
            collective_id=0, has_side_effects=True, vmem_limit_bytes=60 * 1024 * 1024
        ),
    )(
        prompt_states,
        kv_weight,
        prompt_segments,
        page_dest,
        new_slot,
        cache_keys,
        cache_values,
        decode_queries,
        request_pages,
        context_lengths,
        out_weight,
    )


def rotate(key_heads, positions):
    half_width = key_heads.shape[-1] // 2
    frequency = rope_base ** (
        -(jnp.arange(half_width, dtype=jnp.float32) * 2.0) / key_heads.shape[-1]
    )
    angles = positions.astype(jnp.float32)[:, None] * frequency[None, :]
    cosine = jnp.cos(angles)[:, None, :]
    sine_part = jnp.sin(angles)[:, None, :]
    lower_half = key_heads[..., :half_width]
    upper_half = key_heads[..., half_width:]
    return jnp.concatenate(
        [
            lower_half * cosine - upper_half * sine_part,
            upper_half * cosine + lower_half * sine_part,
        ],
        axis=-1,
    )


def page_partials(owned_queries, key_pages, value_pages, page_limit):
    page_count, head_count, page_width, head_depth = key_pages.shape
    grouped = owned_queries.reshape(page_count, head_count, -1, head_depth)
    scores = jnp.einsum(
        "pgqd,pgtd->pgqt", grouped, key_pages, preferred_element_type=jnp.float32
    ) * (1.0 / math.sqrt(head_depth))
    is_live = jnp.arange(page_width)[None, None, None, :] < page_limit[:, None, None, None]
    page_max = jnp.max(jnp.where(is_live, scores, neg_fill), axis=-1)
    weights = jnp.exp(jnp.where(is_live, scores - page_max[..., None], neg_fill)).astype(
        jnp.bfloat16
    )
    page_sum = jnp.sum(weights.astype(jnp.float32), axis=-1)
    page_acc = jnp.einsum(
        "pgqt,pgtd->pgqd", weights, value_pages, preferred_element_type=jnp.float32
    )
    all_heads = head_count * grouped.shape[2]
    return (
        page_max.reshape(page_count, all_heads),
        page_sum.reshape(page_count, all_heads),
        page_acc.reshape(page_count, all_heads, head_depth),
    )


def fold_requests(owned_by, page_max, page_sum, page_acc):
    largest = jnp.max(jnp.where(owned_by[:, :, None], page_max[None], neg_fill), axis=1)
    factor = jnp.where(owned_by[:, :, None], jnp.exp(page_max[None] - largest[:, None, :]), 0.0)
    grand_sum = jnp.sum(factor * page_sum[None], axis=1)
    numerator = jnp.einsum("bsh,shd->bhd", factor, page_acc, precision=lax.Precision.HIGHEST)
    return (largest, grand_sum, numerator)


def finish(exchanged):
    maxima, partial_sums, partial_numer = exchanged
    largest = jnp.max(maxima, axis=0)
    factor = jnp.exp(maxima - largest[None])
    grand_sum = jnp.sum(factor * partial_sums, axis=0)
    summed = jnp.sum(factor[..., None] * partial_numer, axis=0)
    return (summed / grand_sum[..., None]).astype(jnp.bfloat16).reshape(summed.shape[0], -1)


def local(
    prompt_states,
    kv_weight,
    prompt_segments,
    page_dest,
    new_slot,
    cache_keys,
    cache_values,
    decode_queries,
    request_pages,
    context_lengths,
    out_weight,
):
    rank_count = lax.axis_size("tp")
    my_rank = lax.axis_index("tp")
    tokens = prompt_states.shape[0]
    share_len = tokens // rank_count
    kv_sum = lax.psum_scatter(
        jnp.dot(prompt_states, kv_weight, preferred_element_type=jnp.float32).astype(jnp.bfloat16),
        "tp",
        scatter_dimension=0,
        tiled=True,
    ).astype(jnp.float32)
    segments = prompt_segments[0]
    own_segments = lax.dynamic_slice_in_dim(segments, my_rank * share_len, share_len)
    token_index = my_rank * share_len + jnp.arange(share_len, dtype=jnp.int32)
    earlier = (segments[None, :] == own_segments[:, None]) & (
        jnp.arange(tokens, dtype=jnp.int32)[None, :] < token_index[:, None]
    )
    positions = jnp.sum(earlier.astype(jnp.int32), axis=1)
    kv_sum = kv_sum.reshape(share_len, 2, KVH, HD)
    new_keys = rotate(kv_sum[:, 0], positions).astype(jnp.bfloat16)
    new_values = kv_sum[:, 1].astype(jnp.bfloat16)
    fresh = jnp.stack([new_keys, new_values], axis=1).reshape(share_len, 2 * KVH * HD)
    page_owner = page_dest[0]
    page_count = page_owner.shape[0]
    arrived = lax.all_gather(fresh, "tp", axis=0, tiled=True)
    arrived = arrived.reshape(page_count, -1)
    pool_keys = cache_keys[0]
    pool_values = cache_values[0]
    pool_len = pool_keys.shape[0]
    page_width = pool_keys.shape[2]
    lands = (page_owner[None, :] == my_rank) & (
        new_slot[0][None, :] == jnp.arange(pool_len, dtype=jnp.int32)[:, None]
    )
    filled = jnp.any(lands, axis=1)
    incoming = jnp.dot(
        lands.astype(jnp.bfloat16), arrived, preferred_element_type=jnp.float32
    ).astype(jnp.bfloat16)
    incoming = incoming.reshape(pool_len, page_width, 2, KVH, HD)
    incoming_keys = incoming[:, :, 0].transpose(0, 2, 1, 3)
    incoming_values = incoming[:, :, 1].transpose(0, 2, 1, 3)
    slot_ids = my_rank * pool_len + jnp.arange(pool_len, dtype=jnp.int32)
    page_lists = request_pages[0]
    lengths = context_lengths[0]
    longest = page_lists.shape[1]
    matches = page_lists[:, :, None] == slot_ids[None, None, :]
    limits = lengths[:, None] - jnp.arange(longest, dtype=jnp.int32)[None, :] * page_width
    slot_limit = jnp.sum(jnp.where(matches, limits[:, :, None], 0), axis=(0, 1))
    owned_by = jnp.any(matches, axis=1)
    queries = decode_queries[0]
    owned_queries = jnp.dot(
        owned_by.T.astype(jnp.bfloat16), queries, preferred_element_type=jnp.float32
    ).astype(jnp.bfloat16)
    pool_keys = jnp.where(filled[:, None, None, None], incoming_keys, pool_keys)
    pool_values = jnp.where(filled[:, None, None, None], incoming_values, pool_values)
    page_max, page_sum, page_acc = page_partials(owned_queries, pool_keys, pool_values, slot_limit)
    largest, grand_sum, numerator = fold_requests(owned_by, page_max, page_sum, page_acc)
    head_part = finish(
        (
            lax.all_to_all(largest[None], "tp", split_axis=2, concat_axis=0, tiled=True),
            lax.all_to_all(grand_sum[None], "tp", split_axis=2, concat_axis=0, tiled=True),
            lax.all_to_all(numerator[None], "tp", split_axis=2, concat_axis=0, tiled=True),
        )
    )
    attention = lax.all_gather(head_part, "tp", axis=1, tiled=True)
    result = jnp.dot(attention, out_weight, preferred_element_type=jnp.float32).astype(jnp.bfloat16)
    return result[None]


def solution(mesh):
    in_specs = (
        P(("grp", "role"), "tp"),
        P("tp", None),
        P(("grp", "role"), None),
        P(("grp", "role"), None),
        P(("grp", "role"), None),
        P(("grp", "role"), "tp", None, None, None),
        P(("grp", "role"), "tp", None, None, None),
        P(("grp", "role"), None, None),
        P(("grp", "role"), None, None),
        P(("grp", "role"), None),
        P(None, "tp"),
    )
    out_specs = P(("grp", "role"), None, "tp")
    step = fused if mesh.shape["tp"] == KVH else local
    return jax.shard_map(step, mesh=mesh, in_specs=in_specs, out_specs=out_specs, check_vma=False)
```

```python
import functools
import math

import jax
import jax.numpy as jnp
import numpy as np
from jax import lax
from jax.experimental import pallas as pl
from jax.experimental.pallas import tpu as pltpu
from jax.sharding import PartitionSpec as P

KVH = 8
HD = 128


rope_base = 500000.0
neg_fill = -1e30


def cos_turn_coefficients():
    nodes = 0.125 * (1.0 + np.cos((np.arange(400) + 0.5) * np.pi / 400))
    basis = np.polynomial.chebyshev.Chebyshev.fit(
        nodes, np.cos(2.0 * np.pi * np.sqrt(nodes)), 8, domain=[0.0, 0.25]
    )
    return [float(c) for c in basis.convert(kind=np.polynomial.Polynomial).coef]


def rotation_tables(seg_row, tokens, width):
    index = lax.broadcasted_iota(jnp.int32, (tokens, width), 0)
    start = jnp.zeros((tokens, width), jnp.int32)
    for value in range(1, 8):
        first = jnp.sum((seg_row < value).astype(jnp.int32), axis=1, keepdims=True)
        start = jnp.maximum(start, jnp.where(first <= index, first, 0))
    position = (index - start).astype(jnp.float32)
    lane = lax.broadcasted_iota(jnp.int32, (1, width), 1)
    half = width // 2
    low = lane < half
    exponent = jnp.where(low, lane, lane - half).astype(jnp.float32) * (2.0 / width)
    turns = jnp.exp(exponent * (-math.log(rope_base))) * (1.0 / (2.0 * math.pi))
    phase = position * turns
    phase = phase - jnp.round(phase)
    phase = phase - jnp.where(low, 0.0, 0.25)
    phase = phase - jnp.round(phase)
    square = phase * phase
    coefficients = cos_turn_coefficients()
    value = jnp.full_like(square, coefficients[-1])
    for c in coefficients[-2::-1]:
        value = value * square + c
    turned = pltpu.roll(value, half, 1)
    return jnp.where(low, value, turned), jnp.where(low, turned, value)


def fused_kernel(
    ranks,
    x_hbm,
    w_hbm,
    seg_ref,
    dest_ref,
    slot_ref,
    kc_hbm,
    vc_hbm,
    q_ref,
    rp_ref,
    len_ref,
    ow_hbm,
    out_ref,
    x_v,
    wk_v,
    wv_v,
    kc_v,
    vc_v,
    ow_v,
    v_new,
    q_all,
    qp,
    cos_v,
    sin_v,
    live_v,
    s_send,
    s_recv,
    w_all,
    num_send,
    num_recv,
    stat_send,
    stat_recv,
    acc_send,
    acc_recv,
    att_all,
    x_sem,
    wk_sem,
    wv_sem,
    kc_sem,
    vc_sem,
    ow_sem,
    tx,
    rx,
):
    me = lax.axis_index("tp")
    tokens, features = x_v.shape
    pools = kc_hbm.shape[1]
    pages = dest_ref.shape[1]
    page = kc_hbm.shape[3]
    requests = q_ref.shape[1]
    group = q_ref.shape[2] // (KVH * HD)
    rows = group * requests
    chunk = ow_v.shape[1]
    scale = 1.0 / math.sqrt(HD)
    halves = KVH // 2

    barrier = pltpu.get_barrier_semaphore()
    for d in range(1, ranks):
        pl.semaphore_signal(barrier, inc=1, device_id={"tp": lax.rem(me + d, ranks)})

    def pair_of(i):
        return lax.rem(me // 2 + 1 + i, halves)

    def head_of(i):
        return lax.rem(me + 1 + i, ranks)

    def x_copy():
        return pltpu.make_async_copy(x_hbm, x_v, x_sem)

    def wk_copy(i):
        return pltpu.make_async_copy(
            w_hbm.at[:, pl.ds(pl.multiple_of(pair_of(i) * (2 * HD), 2 * HD), 2 * HD)],
            wk_v.at[i],
            wk_sem.at[i],
        )

    def wv_copy(i):
        return pltpu.make_async_copy(
            w_hbm.at[:, pl.ds(pl.multiple_of((halves + i) * (2 * HD), 2 * HD), 2 * HD)],
            wv_v.at[i],
            wv_sem.at[i],
        )

    def kc_copy(i):
        return pltpu.make_async_copy(
            kc_hbm.at[0, i], kc_v.at[:, pl.ds(i * page, page), :], kc_sem.at[i]
        )

    def vc_copy(i):
        return pltpu.make_async_copy(
            vc_hbm.at[0, i], vc_v.at[:, pl.ds(i * page, page), :], vc_sem.at[i]
        )

    def ow_copy(i):
        return pltpu.make_async_copy(
            ow_hbm.at[pl.ds(i * chunk, chunk), :], ow_v.at[i], ow_sem.at[i]
        )

    x_copy().start()
    for i in range(halves):
        wk_copy(i).start()

    def remote(kind, src, dst, peer):
        return pltpu.make_async_remote_copy(
            src_ref=src,
            dst_ref=dst,
            send_sem=tx.at[kind, peer],
            recv_sem=rx.at[kind, me],
            device_id={"tp": peer},
        )

    def score_send(peer):
        return remote(0, s_send.at[peer], s_recv.at[me], peer)

    def weight_send(peer):
        return remote(1, w_all.at[me], w_all.at[me], peer)

    def num_copy(peer):
        return remote(2, num_send.at[peer], num_recv.at[me], peer)

    def stat_copy(peer):
        return remote(3, stat_send.at[peer], stat_recv.at[me], peer)

    def acc_copy(peer):
        return remote(4, acc_send.at[peer], acc_recv.at[me], peer)

    def att_copy(peer):
        return remote(5, att_all.at[me], att_all.at[me], peer)

    def arrival(kind, ref, source):
        pltpu.make_async_remote_copy(
            src_ref=ref.at[source],
            dst_ref=ref.at[source],
            send_sem=tx.at[kind, source],
            recv_sem=rx.at[kind, source],
            device_id={"tp": source},
        ).wait_recv()

    lists = rp_ref[0]
    longest = lists.shape[1]
    entry = lax.broadcasted_iota(jnp.int32, (requests, longest), 1)
    request = lax.broadcasted_iota(jnp.int32, (requests, longest), 0)
    length = jnp.zeros((requests, longest), jnp.int32)
    for r in range(requests):
        length = jnp.where(request == r, len_ref[0, r], length)
    limit = length - entry * page

    targets = [dest_ref[0, p] * pools + slot_ref[0, p] for p in range(pages)]
    token = lax.broadcasted_iota(jnp.int32, (requests, page), 1)
    for s in range(pools):
        g = me * pools + s
        kept = jnp.int32(1)
        for p in range(pages):
            kept = jnp.where(targets[p] == g, 0, kept)
        bound = jnp.sum(jnp.where(lists == g, limit * kept, 0), axis=1, keepdims=True)
        live_v[:, s * page : (s + 1) * page] = jnp.where(token < bound, 1.0, 0.0)
    owners, bounds = [], []
    for p in range(pages):
        hit = lists == targets[p]
        owners.append(jnp.sum(jnp.where(hit, request, 0), keepdims=True))
        bounds.append(jnp.sum(jnp.where(hit, limit, 0), keepdims=True))

    q_rows = q_ref[0].astype(jnp.float32)
    lane = lax.broadcasted_iota(jnp.int32, (1, HD), 1)
    sign = jnp.where(lane < HD // 2, 1.0, -1.0)
    pick_row = lax.broadcasted_iota(jnp.int32, (pages * group, rows), 0)
    pick_col = lax.broadcasted_iota(jnp.int32, (pages * group, rows), 1)
    owner_rows = jnp.zeros((pages * group, rows), jnp.int32)
    for p in range(pages):
        owner_rows = jnp.where(pick_row // group == p, owners[p], owner_rows)
    pick = jnp.where(pick_col == (pick_row % group) * requests + owner_rows, 1.0, 0.0).astype(
        jnp.bfloat16
    )
    for h in range(KVH):
        part = jnp.concatenate(
            [
                q_rows[:, (h * group + k) * HD : (h * group + k + 1) * HD]
                for k in range(group)
            ],
            axis=0,
        )
        both = jnp.concatenate([part, pltpu.roll(part, HD // 2, 1) * sign], axis=1).astype(
            jnp.bfloat16
        )
        q_all[h] = both
        qp[h] = jnp.dot(pick, both, preferred_element_type=jnp.float32).astype(jnp.bfloat16)

    cosine, sine = rotation_tables(seg_ref[...], tokens, HD)
    cos_v[...] = cosine
    sin_v[...] = sine

    x_copy().wait()

    @pl.loop(0, halves)
    def _(i):
        wk_copy(i).wait()
        wv_copy(i).start()
        product = jnp.dot(x_v[...], wk_v[i], preferred_element_type=jnp.float32)
        for j in range(2):
            h = pair_of(i) * 2 + j
            keys = product[:, j * HD : (j + 1) * HD]
            turned = jnp.concatenate([keys * cos_v[...], keys * sin_v[...]], axis=1).astype(
                jnp.bfloat16
            )
            scores = lax.dot_general(
                qp[h], turned, (((1,), (1,)), ((), ())), preferred_element_type=jnp.float32
            )
            for p in range(pages):
                s_send[h, :, p * page : (p + 1) * page] = (
                    scores[p * group : (p + 1) * group, p * page : (p + 1) * page] * scale
                )

        @pl.when(i == 0)
        def _():
            pl.semaphore_wait(barrier, ranks - 1)

        for j in range(2):
            h = pair_of(i) * 2 + j

            @pl.when(h != me)
            def _():
                score_send(h).start()

    for i in range(pools):
        kc_copy(i).start()
    for i in range(pools):
        vc_copy(i).start()

    @pl.loop(0, halves)
    def _(i):
        wv_copy(i).wait()
        product = jnp.dot(x_v[...], wv_v[i], preferred_element_type=jnp.float32)
        for j in range(2):
            v_new[i * 2 + j] = product[:, j * HD : (j + 1) * HD].astype(jnp.bfloat16)

    total_scores = s_send[me]
    for d in range(1, ranks):
        source = lax.rem(me + d, ranks)
        arrival(0, s_recv, source)
        total_scores = total_scores + s_recv[source]
    page_token = lax.broadcasted_iota(jnp.int32, (group, page), 1)
    new_max, new_sum = [], []
    for p in range(pages):
        alive = page_token < bounds[p]
        scores = total_scores[:, p * page : (p + 1) * page]
        top = jnp.max(jnp.where(alive, scores, neg_fill), axis=1, keepdims=True)
        weight = jnp.exp(jnp.where(alive, scores - top, neg_fill)).astype(jnp.bfloat16)
        w_all[me, :, p * page : (p + 1) * page] = weight
        new_max.append(top)
        new_sum.append(jnp.sum(weight.astype(jnp.float32), axis=1, keepdims=True))
    for d in range(1, ranks):
        weight_send(lax.rem(me + d, ranks)).start()


    for i in range(pools):
        kc_copy(i).wait()
    for i in range(pools):
        vc_copy(i).wait()
    stat_lane = lax.broadcasted_iota(jnp.int32, (rows, HD), 1)

    def resident(i, stats):
        h = head_of(i)
        ow_copy(i).start()
        scores = (
            lax.dot_general(
                q_all[h][:, :HD],
                kc_v[h],
                (((1,), (1,)), ((), ())),
                preferred_element_type=jnp.float32,
            )
            * scale
        )
        mask = jnp.concatenate([live_v[...]] * group, axis=0) > 0.5
        top = jnp.max(jnp.where(mask, scores, neg_fill), axis=1, keepdims=True)
        weight = jnp.where(mask, jnp.exp(jnp.where(mask, scores - top, 0.0)), 0.0).astype(
            jnp.bfloat16
        )
        total = jnp.sum(weight.astype(jnp.float32), axis=1, keepdims=True)
        num_send[h] = jnp.dot(weight, vc_v[h], preferred_element_type=jnp.float32).astype(
            jnp.bfloat16
        )

        @pl.when(h != me)
        def _():
            num_copy(h).start()

        stats = jnp.where(stat_lane == h, top, stats)
        return jnp.where(stat_lane == h + KVH, total, stats)

    stats = lax.fori_loop(0, KVH, resident, jnp.zeros((rows, HD), jnp.float32))
    padded = jnp.concatenate([stats, jnp.zeros((HD - rows, HD), jnp.float32)], axis=0)
    flipped = jnp.transpose(padded)
    for h in range(KVH):
        stat_send[h, 0:1, :] = flipped[h : h + 1, :]
        stat_send[h, 1:2, :] = flipped[KVH + h : KVH + h + 1, :]
    for d in range(1, ranks):
        stat_copy(lax.rem(me + d, ranks)).start()

    @pl.loop(0, ranks)
    def _(i):
        h = lax.rem(me + i, ranks)

        @pl.when(h != me)
        def _():
            arrival(1, w_all, h)

        weight = w_all[h]
        values = v_new[h]
        acc_send[h] = jnp.concatenate(
            [
                jnp.dot(
                    weight[:, p * page : (p + 1) * page],
                    values[p * page : (p + 1) * page],
                    preferred_element_type=jnp.float32,
                )
                for p in range(pages)
            ],
            axis=0,
        ).astype(jnp.bfloat16)

        @pl.when(h != me)
        def _():
            acc_copy(h).start()

    source_row = lax.broadcasted_iota(jnp.int32, (HD, HD), 0)
    for d in range(1, ranks):
        arrival(3, stat_recv, lax.rem(me + d, ranks))
    maxima = jnp.zeros((HD, HD), jnp.float32)
    for d in range(ranks):
        block = stat_send[me] if d == 0 else stat_recv[lax.rem(me + d, ranks)]
        maxima = jnp.where(source_row == d, block[0:1, :], maxima)
        maxima = jnp.where(source_row == d + ranks, block[1:2, :], maxima)
    columns = jnp.transpose(maxima)[:rows]
    old_max = [columns[:, d : d + 1] for d in range(ranks)]
    old_sum = [columns[:, ranks + d : ranks + d + 1] for d in range(ranks)]
    row_request = lax.broadcasted_iota(jnp.int32, (rows, HD), 0) % requests

    def spread(value):
        wide = jnp.broadcast_to(value, (group, HD))
        return jnp.broadcast_to(wide[:, None, :], (group, requests, HD)).reshape(rows, HD)

    mine = [row_request == owners[p] for p in range(pages)]
    fresh_max = [jnp.where(mine[p], spread(new_max[p]), neg_fill) for p in range(pages)]
    top = fresh_max[0]
    for value in fresh_max[1:] + old_max:
        top = jnp.maximum(top, value)
    total = jnp.zeros((rows, HD), jnp.float32)
    numer = jnp.zeros((rows, HD), jnp.float32)
    for d in range(ranks):
        source = lax.rem(me + d, ranks)
        if d:
            arrival(2, num_recv, source)
        factor = jnp.exp(old_max[d] - top)
        total = total + factor * old_sum[d]
        block = num_send[me] if d == 0 else num_recv[source]
        numer = numer + factor * block.astype(jnp.float32)
    fresh_factor = [
        jnp.where(mine[p], jnp.exp(fresh_max[p] - top), 0.0) for p in range(pages)
    ]
    for p in range(pages):
        total = total + fresh_factor[p] * spread(new_sum[p])
    fresh_acc = acc_send[me].astype(jnp.float32)
    for d in range(1, ranks):
        source = lax.rem(me + d, ranks)
        arrival(4, acc_recv, source)
        fresh_acc = fresh_acc + acc_recv[source].astype(jnp.float32)
    for p in range(pages):
        numer = numer + fresh_factor[p] * spread(fresh_acc[p * group : (p + 1) * group])
    joined = (numer / total).astype(jnp.bfloat16)
    for k in range(group):
        att_all[me, :, k * HD : (k + 1) * HD] = joined[k * requests : (k + 1) * requests]
    for d in range(1, ranks):
        att_copy(lax.rem(me + d, ranks)).start()

    for i in range(ranks):
        ow_copy(i).wait()

    def project(i, result):
        source = lax.rem(me + i, ranks)

        @pl.when(source != me)
        def _():
            arrival(5, att_all, source)

        return result + jnp.dot(
            att_all[source], ow_v[source], preferred_element_type=jnp.float32
        )

    result = lax.fori_loop(
        0, ranks, project, jnp.zeros((requests, ow_v.shape[2]), jnp.float32)
    )
    out_ref[0] = result.astype(out_ref.dtype)

    for d in range(1, ranks):
        peer = lax.rem(me + d, ranks)
        score_send(peer).wait_send()
        weight_send(peer).wait_send()
        num_copy(peer).wait_send()
        stat_copy(peer).wait_send()
        acc_copy(peer).wait_send()
        att_copy(peer).wait_send()


def fused(
    prompt_states,
    kv_weight,
    prompt_segments,
    page_dest,
    new_slot,
    cache_keys,
    cache_values,
    decode_queries,
    request_pages,
    context_lengths,
    out_weight,
):
    ranks = lax.axis_size("tp")
    tokens, features = prompt_states.shape
    pools, page = cache_keys.shape[1], cache_keys.shape[3]
    pages = page_dest.shape[1]
    requests = decode_queries.shape[1]
    group = decode_queries.shape[2] // (KVH * HD)
    rows = group * requests
    chunk = out_weight.shape[0] // ranks
    width = out_weight.shape[1]
    half = KVH // 2
    vmem = pl.BlockSpec(memory_space=pltpu.VMEM)
    smem = pl.BlockSpec(memory_space=pltpu.SMEM)
    hbm = pl.BlockSpec(memory_space=pl.ANY)
    bf16, f32 = jnp.bfloat16, jnp.float32
    return pl.pallas_call(
        functools.partial(fused_kernel, ranks),
        out_shape=jax.ShapeDtypeStruct((1, requests, width), bf16),
        in_specs=[hbm, hbm, vmem, smem, smem, hbm, hbm, vmem, vmem, smem, hbm],
        out_specs=vmem,
        scratch_shapes=[
            pltpu.VMEM((tokens, features), bf16),
            pltpu.VMEM((half, features, 2 * HD), bf16),
            pltpu.VMEM((half, features, 2 * HD), bf16),
            pltpu.VMEM((KVH, pools * page, HD), bf16),
            pltpu.VMEM((KVH, pools * page, HD), bf16),
            pltpu.VMEM((ranks, chunk, width), bf16),
            pltpu.VMEM((KVH, tokens, HD), bf16),
            pltpu.VMEM((KVH, rows, 2 * HD), bf16),
            pltpu.VMEM((KVH, pages * group, 2 * HD), bf16),
            pltpu.VMEM((tokens, HD), f32),
            pltpu.VMEM((tokens, HD), f32),
            pltpu.VMEM((requests, pools * page), f32),
            pltpu.VMEM((ranks, group, tokens), f32),
            pltpu.VMEM((ranks, group, tokens), f32),
            pltpu.VMEM((ranks, group, tokens), bf16),
            pltpu.VMEM((ranks, rows, HD), bf16),
            pltpu.VMEM((ranks, rows, HD), bf16),
            pltpu.VMEM((ranks, 8, HD), f32),
            pltpu.VMEM((ranks, 8, HD), f32),
            pltpu.VMEM((ranks, pages * group, HD), bf16),
            pltpu.VMEM((ranks, pages * group, HD), bf16),
            pltpu.VMEM((ranks, requests, chunk), bf16),
            pltpu.SemaphoreType.DMA,
            pltpu.SemaphoreType.DMA((half,)),
            pltpu.SemaphoreType.DMA((half,)),
            pltpu.SemaphoreType.DMA((pools,)),
            pltpu.SemaphoreType.DMA((pools,)),
            pltpu.SemaphoreType.DMA((ranks,)),
            pltpu.SemaphoreType.DMA((6, ranks)),
            pltpu.SemaphoreType.DMA((6, ranks)),
        ],
        compiler_params=pltpu.CompilerParams(
            collective_id=0, has_side_effects=True, vmem_limit_bytes=60 * 1024 * 1024
        ),
    )(
        prompt_states,
        kv_weight,
        prompt_segments,
        page_dest,
        new_slot,
        cache_keys,
        cache_values,
        decode_queries,
        request_pages,
        context_lengths,
        out_weight,
    )


def rotate(key_heads, positions):
    half_width = key_heads.shape[-1] // 2
    frequency = rope_base ** (
        -(jnp.arange(half_width, dtype=jnp.float32) * 2.0) / key_heads.shape[-1]
    )
    angles = positions.astype(jnp.float32)[:, None] * frequency[None, :]
    cosine = jnp.cos(angles)[:, None, :]
    sine_part = jnp.sin(angles)[:, None, :]
    lower_half = key_heads[..., :half_width]
    upper_half = key_heads[..., half_width:]
    return jnp.concatenate(
        [
            lower_half * cosine - upper_half * sine_part,
            upper_half * cosine + lower_half * sine_part,
        ],
        axis=-1,
    )


def page_partials(owned_queries, key_pages, value_pages, page_limit):
    page_count, head_count, page_width, head_depth = key_pages.shape
    grouped = owned_queries.reshape(page_count, head_count, -1, head_depth)
    scores = jnp.einsum(
        "pgqd,pgtd->pgqt", grouped, key_pages, preferred_element_type=jnp.float32
    ) * (1.0 / math.sqrt(head_depth))
    is_live = jnp.arange(page_width)[None, None, None, :] < page_limit[:, None, None, None]
    page_max = jnp.max(jnp.where(is_live, scores, neg_fill), axis=-1)
    weights = jnp.exp(jnp.where(is_live, scores - page_max[..., None], neg_fill)).astype(
        jnp.bfloat16
    )
    page_sum = jnp.sum(weights.astype(jnp.float32), axis=-1)
    page_acc = jnp.einsum(
        "pgqt,pgtd->pgqd", weights, value_pages, preferred_element_type=jnp.float32
    )
    all_heads = head_count * grouped.shape[2]
    return (
        page_max.reshape(page_count, all_heads),
        page_sum.reshape(page_count, all_heads),
        page_acc.reshape(page_count, all_heads, head_depth),
    )


def fold_requests(owned_by, page_max, page_sum, page_acc):
    largest = jnp.max(jnp.where(owned_by[:, :, None], page_max[None], neg_fill), axis=1)
    factor = jnp.where(owned_by[:, :, None], jnp.exp(page_max[None] - largest[:, None, :]), 0.0)
    grand_sum = jnp.sum(factor * page_sum[None], axis=1)
    numerator = jnp.einsum("bsh,shd->bhd", factor, page_acc, precision=lax.Precision.HIGHEST)
    return (largest, grand_sum, numerator)


def finish(exchanged):
    maxima, partial_sums, partial_numer = exchanged
    largest = jnp.max(maxima, axis=0)
    factor = jnp.exp(maxima - largest[None])
    grand_sum = jnp.sum(factor * partial_sums, axis=0)
    summed = jnp.sum(factor[..., None] * partial_numer, axis=0)
    return (summed / grand_sum[..., None]).astype(jnp.bfloat16).reshape(summed.shape[0], -1)


def local(
    prompt_states,
    kv_weight,
    prompt_segments,
    page_dest,
    new_slot,
    cache_keys,
    cache_values,
    decode_queries,
    request_pages,
    context_lengths,
    out_weight,
):
    rank_count = lax.axis_size("tp")
    my_rank = lax.axis_index("tp")
    tokens = prompt_states.shape[0]
    share_len = tokens // rank_count
    kv_sum = lax.psum_scatter(
        jnp.dot(prompt_states, kv_weight, preferred_element_type=jnp.float32).astype(jnp.bfloat16),
        "tp",
        scatter_dimension=0,
        tiled=True,
    ).astype(jnp.float32)
    segments = prompt_segments[0]
    own_segments = lax.dynamic_slice_in_dim(segments, my_rank * share_len, share_len)
    token_index = my_rank * share_len + jnp.arange(share_len, dtype=jnp.int32)
    earlier = (segments[None, :] == own_segments[:, None]) & (
        jnp.arange(tokens, dtype=jnp.int32)[None, :] < token_index[:, None]
    )
    positions = jnp.sum(earlier.astype(jnp.int32), axis=1)
    kv_sum = kv_sum.reshape(share_len, 2, KVH, HD)
    new_keys = rotate(kv_sum[:, 0], positions).astype(jnp.bfloat16)
    new_values = kv_sum[:, 1].astype(jnp.bfloat16)
    fresh = jnp.stack([new_keys, new_values], axis=1).reshape(share_len, 2 * KVH * HD)
    page_owner = page_dest[0]
    page_count = page_owner.shape[0]
    arrived = lax.all_gather(fresh, "tp", axis=0, tiled=True)
    arrived = arrived.reshape(page_count, -1)
    pool_keys = cache_keys[0]
    pool_values = cache_values[0]
    pool_len = pool_keys.shape[0]
    page_width = pool_keys.shape[2]
    lands = (page_owner[None, :] == my_rank) & (
        new_slot[0][None, :] == jnp.arange(pool_len, dtype=jnp.int32)[:, None]
    )
    filled = jnp.any(lands, axis=1)
    incoming = jnp.dot(
        lands.astype(jnp.bfloat16), arrived, preferred_element_type=jnp.float32
    ).astype(jnp.bfloat16)
    incoming = incoming.reshape(pool_len, page_width, 2, KVH, HD)
    incoming_keys = incoming[:, :, 0].transpose(0, 2, 1, 3)
    incoming_values = incoming[:, :, 1].transpose(0, 2, 1, 3)
    slot_ids = my_rank * pool_len + jnp.arange(pool_len, dtype=jnp.int32)
    page_lists = request_pages[0]
    lengths = context_lengths[0]
    longest = page_lists.shape[1]
    matches = page_lists[:, :, None] == slot_ids[None, None, :]
    limits = lengths[:, None] - jnp.arange(longest, dtype=jnp.int32)[None, :] * page_width
    slot_limit = jnp.sum(jnp.where(matches, limits[:, :, None], 0), axis=(0, 1))
    owned_by = jnp.any(matches, axis=1)
    queries = decode_queries[0]
    owned_queries = jnp.dot(
        owned_by.T.astype(jnp.bfloat16), queries, preferred_element_type=jnp.float32
    ).astype(jnp.bfloat16)
    pool_keys = jnp.where(filled[:, None, None, None], incoming_keys, pool_keys)
    pool_values = jnp.where(filled[:, None, None, None], incoming_values, pool_values)
    page_max, page_sum, page_acc = page_partials(owned_queries, pool_keys, pool_values, slot_limit)
    largest, grand_sum, numerator = fold_requests(owned_by, page_max, page_sum, page_acc)
    head_part = finish(
        (
            lax.all_to_all(largest[None], "tp", split_axis=2, concat_axis=0, tiled=True),
            lax.all_to_all(grand_sum[None], "tp", split_axis=2, concat_axis=0, tiled=True),
            lax.all_to_all(numerator[None], "tp", split_axis=2, concat_axis=0, tiled=True),
        )
    )
    attention = lax.all_gather(head_part, "tp", axis=1, tiled=True)
    result = jnp.dot(attention, out_weight, preferred_element_type=jnp.float32).astype(jnp.bfloat16)
    return result[None]


def solution(mesh):
    in_specs = (
        P(("grp", "role"), "tp"),
        P("tp", None),
        P(("grp", "role"), None),
        P(("grp", "role"), None),
        P(("grp", "role"), None),
        P(("grp", "role"), "tp", None, None, None),
        P(("grp", "role"), "tp", None, None, None),
        P(("grp", "role"), None, None),
        P(("grp", "role"), None, None),
        P(("grp", "role"), None),
        P(None, "tp"),
    )
    out_specs = P(("grp", "role"), None, "tp")
    step = fused if mesh.shape["tp"] == KVH else local
    return jax.shard_map(step, mesh=mesh, in_specs=in_specs, out_specs=out_specs, check_vma=False)
```
